32 devices in a mesh: groups: 2 (over x), req: 16 (over z, y, core).
Axes of the slice: x: 2, y: 2, z: 4, core: 2. Of those that a mesh axis runs over, the one named last changes fastest.
Arguments:
- queries: bfloat16 [64, 128, 192], P('groups', 'req'), parts along dimension 0, may hold values from -48 to 48
- absorb_key: bfloat16 [128, 128, 512], P('req'), may hold values from -0.5 to 0.5
- absorb_value: bfloat16 [128, 512, 128], P('req'), may hold values from -0.75 to 0.75
- out_weight: bfloat16 [16384, 5120], P('req'), may hold values from -0.046875 to 0.046875
- latent_cache: bfloat16 [64, 4096, 576], P(('groups', 'req')), parts along dimension 0, may hold values from -12 to 12
- lengths: int32 [64], P(('groups', 'req')), parts along dimension 0, may hold values from 2 to 4096, as said below
- slot_request: int32 [64], P('groups'), parts along dimension 0, may hold values from 0 to 31, each once
Outputs:
- attended: bfloat16 [64, 5120], P(('groups', 'req')), parts along dimension 0
The draws below stay inside these ranges and needn't reach their ends.
There are 2 independent parts, one for each index of `groups`. The reference program is written for one: setup_inputs(seed, part) draws one part's arguments, and reference() takes and returns one part's arrays. A program takes and returns all parts, laid end to end along the dimension named above; an argument that names none is the same for every part. Nothing has to cross between parts.
Inputs may be any that keep to these rules, and one draw needn't show every extreme that they name: Slot j's valid positions are its first lengths[j] ones; some slot of each group holds exactly 4096. `slot_request`: each request stands in exactly one slot.
All inputs are finite; a program needn't handle non-finite values.
Results may differ from the reference program's by a relative error of at most 0.0079.
Values may be sent and summed in bfloat16 or wider, within the bound.
A program may use at most 64 MiB of HBM per device.

```python
import math
import jax
import jax.numpy as jnp
from jax import lax

D = 5120
HEADS = 128
NOPE = 128
ROPE = 64
LATENT = 512
VDIM = 128
CTX = 4096
REQS = 32


def draw_queries(key, part):
    shape = (REQS, HEADS, NOPE + ROPE)
    return jnp.clip(1.5 * jax.random.normal(jax.random.fold_in(key, 2), shape, jnp.float32), -9.0, 9.0).astype(jnp.bfloat16)


def draw_latent_cache(key, part):
    shape = (REQS, CTX, LATENT + ROPE)
    return jnp.clip(jax.random.normal(jax.random.fold_in(key, 4), shape, jnp.float32), -6.0, 6.0).astype(jnp.bfloat16)


def draw_lengths(key, part):
    drawn = jax.random.randint(jax.random.fold_in(key, 5), (REQS,), 2, CTX + 1)
    longest = jax.random.randint(jax.random.fold_in(key, 6), (), 0, REQS)
    slots = jnp.arange(REQS)
    return jnp.where(slots == longest, CTX, drawn).astype(jnp.int32)


def levels(rng, shape, shards, smallest, top_value):
    level = 1.0
    for axis_at, parts in shards:
        draws = jax.random.uniform(jax.random.fold_in(jax.random.fold_in(rng, 6), axis_at), (parts,), jnp.float32, smallest / len(shards), top_value / len(shards))
        level = level * jnp.repeat(jnp.exp(draws), shape[axis_at] // parts).reshape((-1,) + (1,) * (len(shape) - 1 - axis_at))
    return level


def noise(stream_key, extent, scale, limit, pieces=(), held_as=jnp.bfloat16):
    result = scale * jax.random.normal(stream_key, extent, jnp.float32)
    if pieces:
        result = result * levels(stream_key, extent, pieces, -0.22, 0.18)
    return jnp.clip(result, -limit, limit).astype(held_as)


def setup_inputs(seed: int = 0, part: int = 0) -> dict:
    keys = jax.random.split(jax.random.key(seed), 8)
    part_keys = jax.random.split(jax.random.fold_in(keys[7], part), 8)
    queries = draw_queries(jax.random.fold_in(jax.random.fold_in(keys[7], part), 71), part)
    absorb_key = noise(keys[1], (HEADS, NOPE, LATENT), NOPE ** -0.5, 0.5, ((0, 16),))
    absorb_value = noise(keys[2], (HEADS, LATENT, VDIM), (LATENT // 8) ** -0.5, 0.75, ((0, 16),))
    out_weight = noise(keys[3], (HEADS * VDIM, D), (HEADS * VDIM) ** -0.5, 0.046875, ((0, 16),))
    latent_cache = draw_latent_cache(jax.random.fold_in(jax.random.fold_in(keys[7], part), 71), part)
    lengths = draw_lengths(jax.random.fold_in(jax.random.fold_in(keys[7], part), 71), part)
    slot_request = jax.random.permutation(part_keys[6], REQS).astype(jnp.int32)
    return dict(queries=queries, absorb_key=absorb_key, absorb_value=absorb_value, out_weight=out_weight, latent_cache=latent_cache, lengths=lengths, slot_request=slot_request)


def attend_slot(absorbed_row, cache_row, length):
    factor = 1.0 / math.sqrt(NOPE + ROPE)
    scores = jnp.dot(absorbed_row, cache_row.T, preferred_element_type=jnp.float32) * factor
    visible = jnp.arange(CTX) < length
    scores = jnp.where(visible[None, :], scores, -jnp.inf)
    highest = lax.optimization_barrier(jnp.max(scores, axis=1, keepdims=True))
    weights = jnp.exp(scores - highest)
    probs = (weights / lax.optimization_barrier(jnp.sum(weights, axis=1, keepdims=True))).astype(jnp.bfloat16)
    return jnp.dot(probs, cache_row[:, :LATENT], preferred_element_type=jnp.float32).astype(jnp.bfloat16)

def reference(queries, absorb_key, absorb_value, out_weight, latent_cache, lengths, slot_request):
    ordered = jnp.take(queries, slot_request, axis=0)
    lifted = jnp.einsum('jhn,hnc->jhc', ordered[:, :, :NOPE].astype(jnp.float32), absorb_key.astype(jnp.float32))
    absorbed = jnp.concatenate([lifted, ordered[:, :, NOPE:].astype(jnp.float32)], axis=2).astype(jnp.bfloat16)
    latent = lax.map(lambda item: attend_slot(item[0], item[1], item[2]), (absorbed, latent_cache, lengths))
    values = jnp.einsum('jhc,hcv->jhv', latent.astype(jnp.float32), absorb_value.astype(jnp.float32)).astype(jnp.bfloat16)
    flattened = values.reshape(REQS, HEADS * VDIM)
    return jnp.dot(flattened, out_weight, preferred_element_type=jnp.float32).astype(jnp.bfloat16)
```

```python
import functools
import math

import jax
import jax.numpy as jnp
from jax import lax
from jax.experimental import pallas as pl
from jax.experimental.pallas import tpu as pltpu
from jax.sharding import PartitionSpec as P

MESH = pl.DeviceIdType.MESH
LANES = 128
CORES = 2
SCORE_TILE = 1024
COLUMNS = 2


def pieces_of(slots, heads):
    whole = [(s, 0, heads) for s in range(slots - 1)]
    return whole + [(slots - 1, 0, heads)]


def far_first(mine, count, width):
    block, place, blocks = lax.div(mine, width), lax.rem(mine, width), count // width
    low = (block < blocks // 2).astype(jnp.int32)
    for i in range(blocks - 1):
        down = blocks - 1 - i - (blocks - 1 - i <= block).astype(jnp.int32)
        up = i + (i >= block).astype(jnp.int32)
        chosen = low * down + (1 - low) * up
        for j in range(width):
            yield chosen * width + lax.rem(place + j, width)
    for j in range(1, width):
        yield block * width + lax.rem(place + j, width)


def kernel(n, pieces, request_hbm, length_hbm, query_hbm, key_hbm, value_hbm, weight_hbm, cache_hbm, out_ref, *scratch):
    parts = len(pieces)
    scratch = list(scratch)
    take = lambda count: [scratch.pop(0) for _ in range(count)]
    request_ref, length_ref, query_ref, key, value, weight, cache = take(7)
    query_rows, rotary_rows, absorbed_rows, slot_rows, scores, latent_rows, returned_rows = take(7)
    absorbed_out, absorbed_in, latent_out, latent_in = take(parts), take(parts), take(parts), take(parts)
    carried, partial, partner_rows, partial_out, partial_in = take(5)
    small_sem, load_sem, send_a, recv_a, send_b, recv_b, send_p, recv_p, send_c, recv_c = take(10)

    requests, heads, width = query_ref.shape
    nope, latent = key_hbm.shape[1:]
    vdim = value_hbm.shape[2]
    slots, _, context = cache_hbm.shape
    rope = width - nope
    lanes = latent // LANES
    chips = n // CORES
    me = lax.axis_index("req")

    barrier = pltpu.get_barrier_semaphore()

    for k in range(1, n):
        pl.semaphore_signal(
            barrier, inc=1, device_id={"req": lax.rem(me + k, n)}, device_id_type=MESH
        )

    small = [
        pltpu.make_async_copy(source, into, small_sem.at[i])
        for i, (source, into) in enumerate(
            [(request_hbm, request_ref), (query_hbm, query_ref), (length_hbm, length_ref)]
        )
    ]
    for load in small:
        load.start()
    load_key = pltpu.make_async_copy(key_hbm, key, load_sem.at[0])
    load_value = pltpu.make_async_copy(value_hbm, value, load_sem.at[1])
    load_weight = pltpu.make_async_copy(weight_hbm, weight, load_sem.at[2])
    load_cache = [
        pltpu.make_async_copy(cache_hbm.at[s], cache.at[s], load_sem.at[3 + s])
        for s in range(slots)
    ]
    load_key.start()
    load_cache[0].start()

    for load in small:
        load.wait()
    for j in range(requests):
        row = query_ref[request_ref[j]].astype(jnp.float32)
        query_rows[j * heads : (j + 1) * heads, :] = row[:, :nope]
        rotary_rows[j * heads : (j + 1) * heads, :] = row[:, nope:]
    load_key.wait()
    for s in range(1, slots):
        load_cache[s].start()
    load_value.start()
    load_weight.start()
    for h in range(heads):
        picked = query_rows[pl.ds(h, requests, stride=heads), :].astype(jnp.bfloat16)
        lifted = jnp.dot(picked, key[h], preferred_element_type=jnp.float32)
        for l in range(lanes):
            absorbed_rows[l, pl.ds(h, requests, stride=heads), :] = lifted[
                :, l * LANES : (l + 1) * LANES
            ]

    def exchange(out, into, send_sem, recv_sem, stride=1):
        mine, count = lax.div(me, stride), n // stride

        def copy(to, source, block):
            return pltpu.make_async_remote_copy(
                src_ref=out.at[block + (to,)],
                dst_ref=into.at[block + (source,)],
                send_sem=send_sem,
                recv_sem=recv_sem,
                device_id={"req": to * stride + lax.rem(me, stride)},
                device_id_type=MESH,
            )

        def start(*block):
            for to in far_first(mine, count, 2 * CORES // stride):
                copy(to, mine, block).start()

        def others(ref):
            block = ref.at[(slice(None),) * (len(ref.shape) - 3) + (pl.ds(0, count - 1),)]
            return pltpu.make_async_copy(block, block, recv_sem if ref is into else send_sem)

        def arrive():
            others(into).wait()

        def leave():
            others(out).wait()

        return start, arrive, leave

    queries_of = [
        exchange(absorbed_out[p], absorbed_in[p], send_a.at[p], recv_a.at[p]) for p in range(parts)
    ]
    latents_of = [
        exchange(latent_out[p], latent_in[p], send_b.at[p], recv_b.at[p]) for p in range(parts)
    ]
    partials_of = [
        exchange(partial_out.at[s], partial_in.at[s], send_c.at[s], recv_c.at[s], CORES)
        for s in range(slots)
    ]

    for p, (s, first, end) in enumerate(pieces):
        for d in range(n):
            row = (d * slots + s) * heads
            for l in range(lanes):
                absorbed_out[p][d, :, l * LANES : (l + 1) * LANES] = absorbed_rows[
                    l, row + first : row + end, :
                ].astype(jnp.bfloat16)
            if p == 0:
                rotary = [
                    rotary_rows[(d * slots + i) * heads : (d * slots + i + 1) * heads, :]
                    for i in range(slots)
                ]
                absorbed_out[p][d, :, latent:] = jnp.concatenate(rotary, axis=1).astype(jnp.bfloat16)
        if p == 0:
            pl.semaphore_wait(barrier, n - 1)
        queries_of[p][0]()
        absorbed_in[p][me] = absorbed_out[p][me]

    scale = math.log2(math.e) / math.sqrt(width)
    for p, (s, first, end) in enumerate(pieces):
        count = end - first
        rows = n * count
        queries_of[p][1]()
        for i in range(n):
            slot_rows[i * count : (i + 1) * count, :latent] = absorbed_in[p][i, :, :latent].astype(
                jnp.float32
            )
            rotary = absorbed_in[0][i, :, latent:].astype(jnp.float32)
            slot_rows[i * count : (i + 1) * count, latent:] = rotary[
                first:end, s * rope : (s + 1) * rope
            ]
        query = slot_rows[:rows, :].astype(jnp.bfloat16)
        if first == 0:
            load_cache[s].wait()
        length = length_ref[s]
        highest = None
        for t in range(0, context, SCORE_TILE):
            score = jnp.dot(
                query, cache[s, :, t : t + SCORE_TILE], preferred_element_type=jnp.float32
            )
            position = t + lax.broadcasted_iota(jnp.int32, (1, SCORE_TILE), 1)
            score = jnp.where(position < length, score, -jnp.inf)
            scores[:rows, t : t + SCORE_TILE] = score
            top = jnp.max(score, axis=1, keepdims=True)
            highest = top if highest is None else jnp.maximum(highest, top)
        total, mixed = None, None
        for t in range(0, context, SCORE_TILE):
            prob = jnp.exp2((scores[:rows, t : t + SCORE_TILE] - highest) * scale)
            part = jnp.sum(prob, axis=1, keepdims=True)
            product = lax.dot_general(
                prob.astype(jnp.bfloat16),
                cache[s, :latent, t : t + SCORE_TILE],
                (((1,), (1,)), ((), ())),
                preferred_element_type=jnp.float32,
            )
            total = part if total is None else total + part
            mixed = product if mixed is None else mixed + product
        latent_rows[:rows, :] = mixed / total
        for i in range(n):
            latent_out[p][i] = latent_rows[i * count : (i + 1) * count, :].astype(jnp.bfloat16)
        latents_of[p][0]()
        latent_in[p][me] = latent_out[p][me]

    core, chip = lax.rem(me, CORES), lax.div(me, CORES)
    model = out_ref.shape[1]
    span = model // COLUMNS
    half = span // 2

    def pair(s, k):
        return pltpu.make_async_remote_copy(
            src_ref=partial.at[s, k, CORES - 1 - core],
            dst_ref=partner_rows.at[s, k],
            send_sem=send_p.at[s, k],
            recv_sem=recv_p.at[s, k],
            device_id={"req": me + CORES - 1 - 2 * core},
            device_id_type=MESH,
        )

    waiting = []

    def finish(s, k):
        pair(s, k).wait_recv()
        chip_rows = partial[s, k, core] + partner_rows[s, k]
        for e in range(chips):
            partial_out[s, k, e] = jnp.concatenate(
                [chip_rows[e : e + 1, :half], chip_rows[e : e + 1, half:]], axis=0
            ).astype(jnp.bfloat16)
        partials_of[s][0](k)
        partial_in[s, k, chip] = partial_out[s, k, chip]

    load_value.wait()
    load_weight.wait()
    for p, (s, first, end) in enumerate(pieces):
        count = end - first
        latents_of[p][1]()
        for d in range(n):
            row = ((d % CORES) * chips + d // CORES) * count
            for l in range(lanes):
                returned_rows[l, row : row + count, :] = latent_in[p][
                    d, :, l * LANES : (l + 1) * LANES
                ].astype(jnp.float32)
        values = []
        for h in range(count):
            picked = jnp.concatenate(
                [returned_rows[l, pl.ds(h, n, stride=count), :] for l in range(lanes)], axis=1
            ).astype(jnp.bfloat16)
            values.append(
                jnp.dot(picked, value[first + h], preferred_element_type=jnp.float32).astype(
                    jnp.bfloat16
                )
            )
        values = jnp.concatenate(values, axis=1)
        for k in range(COLUMNS):
            product = jnp.dot(
                values,
                weight[first * vdim : end * vdim, k * span : (k + 1) * span],
                preferred_element_type=jnp.float32,
            )
            if first > 0:
                product = product + carried[:, k * span : (k + 1) * span]
            if end < heads:
                carried[:, k * span : (k + 1) * span] = product
            else:
                for c in range(CORES):
                    partial[s, k, c] = product[c * chips : (c + 1) * chips]
                pair(s, k).start()
                waiting.append((s, k))
            while len(waiting) > 1 or (waiting and end < heads):
                finish(*waiting.pop(0))
    while waiting:
        finish(*waiting.pop(0))

    for s in range(slots):
        partials_of[s][1]()
    for k in range(COLUMNS):
        sums = []
        for s in range(slots):
            summed = partial_in[s, k, 0].astype(jnp.float32)
            for e in range(1, chips):
                summed = summed + partial_in[s, k, e].astype(jnp.float32)
            sums.append(summed)
        for c in range(2):
            at = k * span + c * half
            out_ref[:, at : at + half] = jnp.concatenate(
                [summed[c : c + 1] for summed in sums], axis=0
            ).astype(jnp.bfloat16)
    for s in range(slots):
        for k in range(COLUMNS):
            pair(s, k).wait_send()
    for pending in queries_of + latents_of + partials_of:
        pending[2]()


def on_device(n, queries, absorb_key, absorb_value, out_weight, latent_cache, lengths, slot_request):
    cache = jnp.swapaxes(latent_cache, 1, 2)
    requests, heads, width = queries.shape
    slots, key_width, context = cache.shape
    nope, latent = absorb_key.shape[1:]
    model = out_weight.shape[1]
    rows = requests * heads
    chips = n // CORES
    pieces = pieces_of(slots, heads)
    span = model // COLUMNS
    vmem, anywhere = (pl.BlockSpec(memory_space=space) for space in (pltpu.VMEM, pltpu.HBM))
    low, wide = jnp.bfloat16, jnp.float32
    absorbed = [
        pltpu.VMEM((n, end - first, latent + (slots * (width - nope) if p == 0 else 0)), low)
        for p, (_, first, end) in enumerate(pieces)
    ]
    mixed = [pltpu.VMEM((n, end - first, latent), low) for _, first, end in pieces]
    per_piece = pltpu.SemaphoreType.DMA((len(pieces),))
    return pl.pallas_call(
        functools.partial(kernel, n, pieces),
        out_shape=jax.ShapeDtypeStruct((slots, model), low),
        in_specs=[anywhere] * 7,
        out_specs=vmem,
        scratch_shapes=[
            pltpu.SMEM(slot_request.shape, jnp.int32),
            pltpu.SMEM(lengths.shape, jnp.int32),
            pltpu.VMEM(queries.shape, low),
            pltpu.VMEM(absorb_key.shape, low),
            pltpu.VMEM(absorb_value.shape, low),
            pltpu.VMEM(out_weight.shape, low),
            pltpu.VMEM(cache.shape, low),
            pltpu.VMEM((rows, nope), wide),
            pltpu.VMEM((rows, width - nope), wide),
            pltpu.VMEM((latent // LANES, rows, LANES), wide),
            pltpu.VMEM((n * heads, key_width), wide),
            pltpu.VMEM((n * heads, context), wide),
            pltpu.VMEM((n * heads, latent), wide),
            pltpu.VMEM((latent // LANES, n * heads, LANES), wide),
            *absorbed,
            *absorbed,
            *mixed,
            *mixed,
            pltpu.VMEM((n, model), wide),
            pltpu.VMEM((slots, COLUMNS, CORES, chips, span), wide),
            pltpu.VMEM((slots, COLUMNS, chips, span), wide),
            pltpu.VMEM((slots, COLUMNS, chips, 2, span // 2), low),
            pltpu.VMEM((slots, COLUMNS, chips, 2, span // 2), low),
            pltpu.SemaphoreType.DMA((3,)),
            pltpu.SemaphoreType.DMA((3 + slots,)),
            per_piece,
            per_piece,
            per_piece,
            per_piece,
            pltpu.SemaphoreType.DMA((slots, COLUMNS)),
            pltpu.SemaphoreType.DMA((slots, COLUMNS)),
            pltpu.SemaphoreType.DMA((slots,)),
            pltpu.SemaphoreType.DMA((slots,)),
        ],
        compiler_params=pltpu.CompilerParams(
            collective_id=0, has_side_effects=True, vmem_limit_bytes=56000 * 1000
        ),
        name="decode",
    )(
        *(
            pltpu.with_memory_space_constraint(operand, pltpu.HBM)
            for operand in (slot_request, lengths, queries, absorb_key, absorb_value, out_weight, cache)
        )
    )


def solution(mesh):
    return jax.shard_map(
        functools.partial(on_device, mesh.shape["req"]),
        mesh=mesh,
        in_specs=(
            P("groups", "req", None),
            P("req", None, None),
            P("req", None, None),
            P("req", None),
            P(("groups", "req"), None, None),
            P(("groups", "req")),
            P("groups"),
        ),
        out_specs=P(("groups", "req"), None),
        check_vma=False,
    )
```

```python
import functools
import math

import jax
import jax.numpy as jnp
from jax import lax
from jax.experimental import pallas as pl
from jax.experimental.pallas import tpu as pltpu
from jax.sharding import PartitionSpec as P

MESH = pl.DeviceIdType.MESH
LANES = 128
CORES = 2
SCORE_TILE = 1024
COLUMNS = 2
STAGES = 4


def pieces_of(slots, heads):
    whole = [(s, 0, heads) for s in range(slots - 1)]
    return whole + [(slots - 1, 0, heads)]


def far_first(mine, count, width, near_edges=False):
    block, place, blocks = lax.div(mine, width), lax.rem(mine, width), count // width
    low = (block < blocks // 2).astype(jnp.int32)
    edge = (block == 0).astype(jnp.int32) + (block == blocks - 1).astype(jnp.int32)
    for step in range(blocks - 1):
        i = lax.rem(step + edge * (blocks - 2), blocks - 1) if near_edges else step
        down = blocks - 1 - i - (blocks - 1 - i <= block).astype(jnp.int32)
        up = i + (i >= block).astype(jnp.int32)
        chosen = low * down + (1 - low) * up
        for j in range(width):
            yield chosen * width + lax.rem(place + j, width)
    for j in range(1, width):
        yield block * width + lax.rem(place + j, width)


def kernel(n, pieces, request_hbm, length_hbm, query_hbm, key_hbm, value_hbm, weight_hbm, cache_hbm, out_ref, *scratch):
    parts = len(pieces)
    scratch = list(scratch)
    take = lambda count: [scratch.pop(0) for _ in range(count)]
    request_ref, length_ref, query_ref, key, value, weight, cache = take(7)
    query_rows, rotary_rows, absorbed_rows, slot_rows, scores, latent_rows, returned_rows = take(7)
    absorbed_out, absorbed_in, latent_out, latent_in = take(parts), take(parts), take(parts), take(parts)
    carried, partial, partner_rows, partial_out, partial_in = take(5)
    small_sem, load_sem, send_a, recv_a, send_b, recv_b, send_p, recv_p, send_c, recv_c = take(10)

    requests, heads, width = query_ref.shape
    nope, latent = key_hbm.shape[1:]
    vdim = value_hbm.shape[2]
    slots, _, context = cache_hbm.shape
    rope = width - nope
    lanes = latent // LANES
    chips = n // CORES
    me = lax.axis_index("req")

    barrier = pltpu.get_barrier_semaphore()

    for k in range(1, n):
        pl.semaphore_signal(
            barrier, inc=1, device_id={"req": lax.rem(me + k, n)}, device_id_type=MESH
        )

    small = [
        pltpu.make_async_copy(source, into, small_sem.at[i])
        for i, (source, into) in enumerate(
            [(request_hbm, request_ref), (query_hbm, query_ref), (length_hbm, length_ref)]
        )
    ]
    for load in small:
        load.start()
    load_key = pltpu.make_async_copy(key_hbm, key, load_sem.at[0])
    load_value = pltpu.make_async_copy(value_hbm, value, load_sem.at[1])
    load_weight = pltpu.make_async_copy(weight_hbm, weight, load_sem.at[2])
    load_cache = [
        pltpu.make_async_copy(cache_hbm.at[s], cache.at[s], load_sem.at[3 + s])
        for s in range(slots)
    ]
    load_key.start()
    load_cache[0].start()

    for load in small:
        load.wait()
    for j in range(requests):
        row = query_ref[request_ref[j]].astype(jnp.float32)
        query_rows[j * heads : (j + 1) * heads, :] = row[:, :nope]
        rotary_rows[j * heads : (j + 1) * heads, :] = row[:, nope:]
    load_key.wait()
    for s in range(1, slots):
        load_cache[s].start()
    load_value.start()
    load_weight.start()
    for h in range(heads):
        picked = query_rows[pl.ds(h, requests, stride=heads), :].astype(jnp.bfloat16)
        lifted = jnp.dot(picked, key[h], preferred_element_type=jnp.float32)
        for l in range(lanes):
            absorbed_rows[l, pl.ds(h, requests, stride=heads), :] = lifted[
                :, l * LANES : (l + 1) * LANES
            ]

    def exchange(out, into, send_sem, recv_sem, stride=1, near_edges=False):
        mine, count = lax.div(me, stride), n // stride

        def copy(to, source, block):
            return pltpu.make_async_remote_copy(
                src_ref=out.at[block + (to,)],
                dst_ref=into.at[block + (source,)],
                send_sem=send_sem,
                recv_sem=recv_sem,
                device_id={"req": to * stride + lax.rem(me, stride)},
                device_id_type=MESH,
            )

        def start(*block):
            for to in far_first(mine, count, 2 * CORES // stride, near_edges):
                copy(to, mine, block).start()

        def others(ref):
            block = ref.at[(slice(None),) * (len(ref.shape) - 3) + (pl.ds(0, count - 1),)]
            return pltpu.make_async_copy(block, block, recv_sem if ref is into else send_sem)

        def arrive():
            others(into).wait()

        def leave():
            others(out).wait()

        return start, arrive, leave

    queries_of = [
        exchange(absorbed_out[p], absorbed_in[p], send_a.at[p], recv_a.at[p], near_edges=p > 0)
        for p in range(parts)
    ]
    latents_of = [
        exchange(latent_out[p], latent_in[p], send_b.at[p], recv_b.at[p])
        for p in range(parts)
    ]
    partials_of = [
        exchange(partial_out.at[s], partial_in.at[s], send_c.at[s], recv_c.at[s], CORES)
        for s in range(slots)
    ]

    for p, (s, first, end) in enumerate(pieces):
        for d in range(n):
            row = (d * slots + s) * heads
            for l in range(lanes):
                absorbed_out[p][d, :, l * LANES : (l + 1) * LANES] = absorbed_rows[
                    l, row + first : row + end, :
                ].astype(jnp.bfloat16)
            if p == 0:
                rotary = [
                    rotary_rows[(d * slots + i) * heads : (d * slots + i + 1) * heads, :]
                    for i in range(slots)
                ]
                absorbed_out[p][d, :, latent:] = jnp.concatenate(rotary, axis=1).astype(jnp.bfloat16)
        if p == 0:
            pl.semaphore_wait(barrier, n - 1)
        queries_of[p][0]()
        absorbed_in[p][me] = absorbed_out[p][me]

    scale = math.log2(math.e) / math.sqrt(width)
    for p, (s, first, end) in enumerate(pieces):
        count = end - first
        rows = n * count
        queries_of[p][1]()
        for i in range(n):
            slot_rows[i * count : (i + 1) * count, :latent] = absorbed_in[p][i, :, :latent].astype(
                jnp.float32
            )
            rotary = absorbed_in[0][i, :, latent:].astype(jnp.float32)
            slot_rows[i * count : (i + 1) * count, latent:] = rotary[
                first:end, s * rope : (s + 1) * rope
            ]
        query = slot_rows[:rows, :].astype(jnp.bfloat16)
        if first == 0:
            load_cache[s].wait()
        length = length_ref[s]
        tops = []
        for t in range(0, context, SCORE_TILE):
            score = jnp.dot(
                query, cache[s, :, t : t + SCORE_TILE], preferred_element_type=jnp.float32
            )
            position = t + lax.broadcasted_iota(jnp.int32, (1, SCORE_TILE), 1)
            score = jnp.where(position < length, score, -jnp.inf)
            scores[:rows, t : t + SCORE_TILE] = score
            tops.append(jnp.max(score, axis=1, keepdims=True))
        highest, total, mixed = None, None, None
        for stage in range(STAGES):
            tiles = range(
                stage * context // STAGES, (stage + 1) * context // STAGES, SCORE_TILE
            )
            top = functools.reduce(jnp.maximum, [tops[t // SCORE_TILE] for t in tiles])
            if highest is not None:
                top = jnp.maximum(highest, top)
                keep = jnp.exp2((highest - top) * scale)
                total, mixed = total * keep, mixed * keep
            highest = top
            for t in tiles:
                prob = jnp.exp2((scores[:rows, t : t + SCORE_TILE] - highest) * scale)
                part = jnp.sum(prob, axis=1, keepdims=True)
                product = lax.dot_general(
                    prob.astype(jnp.bfloat16),
                    cache[s, :latent, t : t + SCORE_TILE],
                    (((1,), (1,)), ((), ())),
                    preferred_element_type=jnp.float32,
                )
                total = part if total is None else total + part
                mixed = product if mixed is None else mixed + product
        latent_rows[:rows, :] = mixed / total
        for i in range(n):
            latent_out[p][i] = latent_rows[i * count : (i + 1) * count, :].astype(jnp.bfloat16)
        latents_of[p][0]()
        latent_in[p][me] = latent_out[p][me]

    core, chip = lax.rem(me, CORES), lax.div(me, CORES)
    model = out_ref.shape[1]
    span = model // COLUMNS
    half = span // 2

    def pair(s, k):
        return pltpu.make_async_remote_copy(
            src_ref=partial.at[s, k, CORES - 1 - core],
            dst_ref=partner_rows.at[s, k],
            send_sem=send_p.at[s, k],
            recv_sem=recv_p.at[s, k],
            device_id={"req": me + CORES - 1 - 2 * core},
            device_id_type=MESH,
        )

    waiting = []

    def finish(s, k):
        pair(s, k).wait_recv()
        chip_rows = partial[s, k, core] + partner_rows[s, k]
        for e in range(chips):
            partial_out[s, k, e] = jnp.concatenate(
                [chip_rows[e : e + 1, :half], chip_rows[e : e + 1, half:]], axis=0
            ).astype(jnp.bfloat16)
        partials_of[s][0](k)
        partial_in[s, k, chip] = partial_out[s, k, chip]

    load_value.wait()
    load_weight.wait()
    for p, (s, first, end) in enumerate(pieces):
        count = end - first
        latents_of[p][1]()
        for d in range(n):
            row = ((d % CORES) * chips + d // CORES) * count
            for l in range(lanes):
                returned_rows[l, row : row + count, :] = latent_in[p][
                    d, :, l * LANES : (l + 1) * LANES
                ].astype(jnp.float32)
        values = []
        for h in range(count):
            picked = jnp.concatenate(
                [returned_rows[l, pl.ds(h, n, stride=count), :] for l in range(lanes)], axis=1
            ).astype(jnp.bfloat16)
            values.append(
                jnp.dot(picked, value[first + h], preferred_element_type=jnp.float32).astype(
                    jnp.bfloat16
                )
            )
        values = jnp.concatenate(values, axis=1)
        for k in range(COLUMNS):
            product = jnp.dot(
                values,
                weight[first * vdim : end * vdim, k * span : (k + 1) * span],
                preferred_element_type=jnp.float32,
            )
            if first > 0:
                product = product + carried[:, k * span : (k + 1) * span]
            if end < heads:
                carried[:, k * span : (k + 1) * span] = product
            else:
                for c in range(CORES):
                    partial[s, k, c] = product[c * chips : (c + 1) * chips]
                pair(s, k).start()
                waiting.append((s, k))
            while len(waiting) > 1 or (waiting and end < heads):
                finish(*waiting.pop(0))
    while waiting:
        finish(*waiting.pop(0))

    for s in range(slots):
        partials_of[s][1]()
    for k in range(COLUMNS):
        sums = []
        for s in range(slots):
            summed = partial_in[s, k, 0].astype(jnp.float32)
            for e in range(1, chips):
                summed = summed + partial_in[s, k, e].astype(jnp.float32)
            sums.append(summed)
        for c in range(2):
            at = k * span + c * half
            out_ref[:, at : at + half] = jnp.concatenate(
                [summed[c : c + 1] for summed in sums], axis=0
            ).astype(jnp.bfloat16)
    for s in range(slots):
        for k in range(COLUMNS):
            pair(s, k).wait_send()
    for pending in queries_of + latents_of + partials_of:
        pending[2]()


def on_device(n, queries, absorb_key, absorb_value, out_weight, latent_cache, lengths, slot_request):
    cache = jnp.swapaxes(latent_cache, 1, 2)
    requests, heads, width = queries.shape
    slots, key_width, context = cache.shape
    nope, latent = absorb_key.shape[1:]
    model = out_weight.shape[1]
    rows = requests * heads
    chips = n // CORES
    pieces = pieces_of(slots, heads)
    span = model // COLUMNS
    vmem, anywhere = (pl.BlockSpec(memory_space=space) for space in (pltpu.VMEM, pltpu.HBM))
    low, wide = jnp.bfloat16, jnp.float32
    absorbed = [
        pltpu.VMEM((n, end - first, latent + (slots * (width - nope) if p == 0 else 0)), low)
        for p, (_, first, end) in enumerate(pieces)
    ]
    mixed = [pltpu.VMEM((n, end - first, latent), low) for _, first, end in pieces]
    per_piece = pltpu.SemaphoreType.DMA((len(pieces),))
    return pl.pallas_call(
        functools.partial(kernel, n, pieces),
        out_shape=jax.ShapeDtypeStruct((slots, model), low),
        in_specs=[anywhere] * 7,
        out_specs=vmem,
        scratch_shapes=[
            pltpu.SMEM(slot_request.shape, jnp.int32),
            pltpu.SMEM(lengths.shape, jnp.int32),
            pltpu.VMEM(queries.shape, low),
            pltpu.VMEM(absorb_key.shape, low),
            pltpu.VMEM(absorb_value.shape, low),
            pltpu.VMEM(out_weight.shape, low),
            pltpu.VMEM(cache.shape, low),
            pltpu.VMEM((rows, nope), wide),
            pltpu.VMEM((rows, width - nope), wide),
            pltpu.VMEM((latent // LANES, rows, LANES), wide),
            pltpu.VMEM((n * heads, key_width), wide),
            pltpu.VMEM((n * heads, context), wide),
            pltpu.VMEM((n * heads, latent), wide),
            pltpu.VMEM((latent // LANES, n * heads, LANES), wide),
            *absorbed,
            *absorbed,
            *mixed,
            *mixed,
            pltpu.VMEM((n, model), wide),
            pltpu.VMEM((slots, COLUMNS, CORES, chips, span), wide),
            pltpu.VMEM((slots, COLUMNS, chips, span), wide),
            pltpu.VMEM((slots, COLUMNS, chips, 2, span // 2), low),
            pltpu.VMEM((slots, COLUMNS, chips, 2, span // 2), low),
            pltpu.SemaphoreType.DMA((3,)),
            pltpu.SemaphoreType.DMA((3 + slots,)),
            per_piece,
            per_piece,
            per_piece,
            per_piece,
            pltpu.SemaphoreType.DMA((slots, COLUMNS)),
            pltpu.SemaphoreType.DMA((slots, COLUMNS)),
            pltpu.SemaphoreType.DMA((slots,)),
            pltpu.SemaphoreType.DMA((slots,)),
        ],
        compiler_params=pltpu.CompilerParams(
            collective_id=0, has_side_effects=True, vmem_limit_bytes=56000 * 1000
        ),
        name="decode",
    )(
        *(
            pltpu.with_memory_space_constraint(operand, pltpu.HBM)
            for operand in (slot_request, lengths, queries, absorb_key, absorb_value, out_weight, cache)
        )
    )


def solution(mesh):
    return jax.shard_map(
        functools.partial(on_device, mesh.shape["req"]),
        mesh=mesh,
        in_specs=(
            P("groups", "req", None),
            P("req", None, None),
            P("req", None, None),
            P("req", None),
            P(("groups", "req"), None, None),
            P(("groups", "req")),
            P("groups"),
        ),
        out_specs=P(("groups", "req"), None),
        check_vma=False,
    )
```

```python
import functools
import math

import jax
import jax.numpy as jnp
from jax import lax
from jax.experimental import pallas as pl
from jax.experimental.pallas import tpu as pltpu
from jax.sharding import PartitionSpec as P

MESH = pl.DeviceIdType.MESH
LANES = 128
CORES = 2
SCORE_TILE = 1024
COLUMNS = 2
STAGES = 4


def pieces_of(slots, heads):
    whole = [(s, 0, heads) for s in range(slots - 1)]
    return whole + [(slots - 1, 0, heads)]


def far_first(mine, count, width, near_edges=False):
    block, place, blocks = lax.div(mine, width), lax.rem(mine, width), count // width
    low = (block < blocks // 2).astype(jnp.int32)
    edge = (block == 0).astype(jnp.int32) + (block == blocks - 1).astype(jnp.int32)
    for step in range(blocks - 1):
        i = lax.rem(step + edge * (blocks - 2), blocks - 1) if near_edges else step
        down = blocks - 1 - i - (blocks - 1 - i <= block).astype(jnp.int32)
        up = i + (i >= block).astype(jnp.int32)
        chosen = low * down + (1 - low) * up
        for j in range(width):
            yield chosen * width + lax.rem(place + j, width)
    for j in range(1, width):
        yield block * width + lax.rem(place + j, width)


def kernel(n, pieces, request_hbm, length_hbm, query_hbm, key_hbm, value_hbm, weight_hbm, cache_hbm, out_ref, *scratch):
    parts = len(pieces)
    scratch = list(scratch)
    take = lambda count: [scratch.pop(0) for _ in range(count)]
    request_ref, length_ref, query_ref, key, value, weight, cache = take(7)
    query_rows, rotary_rows, absorbed_rows, slot_rows, scores, latent_rows, returned_rows = take(7)
    absorbed_out, absorbed_in, latent_out, latent_in = take(parts), take(parts), take(parts), take(parts)
    carried, partial, partner_rows, partial_out, partial_in = take(5)
    small_sem, load_sem, send_a, recv_a, send_b, recv_b, send_p, recv_p, send_c, recv_c = take(10)

    requests, heads, width = query_ref.shape
    nope, latent = key_hbm.shape[1:]
    vdim = value_hbm.shape[2]
    slots, _, context = cache_hbm.shape
    rope = width - nope
    lanes = latent // LANES
    chips = n // CORES
    me = lax.axis_index("req")

    barrier = pltpu.get_barrier_semaphore()

    for k in range(1, n):
        pl.semaphore_signal(
            barrier, inc=1, device_id={"req": lax.rem(me + k, n)}, device_id_type=MESH
        )

    small = [
        pltpu.make_async_copy(source, into, small_sem.at[i])
        for i, (source, into) in enumerate(
            [(request_hbm, request_ref), (query_hbm, query_ref), (length_hbm, length_ref)]
        )
    ]
    for load in small:
        load.start()
    load_key = pltpu.make_async_copy(key_hbm, key, load_sem.at[0])
    load_value = pltpu.make_async_copy(value_hbm, value, load_sem.at[1])
    load_weight = pltpu.make_async_copy(weight_hbm, weight, load_sem.at[2])
    load_cache = [
        pltpu.make_async_copy(cache_hbm.at[s], cache.at[s], load_sem.at[3 + s])
        for s in range(slots)
    ]
    load_key.start()

    for load in small:
        load.wait()
    for j in range(requests):
        row = query_ref[request_ref[j]].astype(jnp.float32)
        query_rows[j * heads : (j + 1) * heads, :] = row[:, :nope]
        rotary_rows[j * heads : (j + 1) * heads, :] = row[:, nope:]
    load_key.wait()
    for load in load_cache:
        load.start()
    load_value.start()
    load_weight.start()
    for h in range(heads):
        picked = query_rows[pl.ds(h, requests, stride=heads), :].astype(jnp.bfloat16)
        lifted = jnp.dot(picked, key[h], preferred_element_type=jnp.float32)
        for l in range(lanes):
            absorbed_rows[l, pl.ds(h, requests, stride=heads), :] = lifted[
                :, l * LANES : (l + 1) * LANES
            ]

    def exchange(out, into, send_sem, recv_sem, stride=1, near_edges=False):
        mine, count = lax.div(me, stride), n // stride

        def copy(to, source, block):
            return pltpu.make_async_remote_copy(
                src_ref=out.at[block + (to,)],
                dst_ref=into.at[block + (source,)],
                send_sem=send_sem,
                recv_sem=recv_sem,
                device_id={"req": to * stride + lax.rem(me, stride)},
                device_id_type=MESH,
            )

        def start(*block):
            for to in far_first(mine, count, 2 * CORES // stride, near_edges):
                copy(to, mine, block).start()

        def others(ref):
            block = ref.at[(slice(None),) * (len(ref.shape) - 3) + (pl.ds(0, count - 1),)]
            return pltpu.make_async_copy(block, block, recv_sem if ref is into else send_sem)

        def arrive():
            others(into).wait()

        def leave():
            others(out).wait()

        return start, arrive, leave

    queries_of = [
        exchange(absorbed_out[p], absorbed_in[p], send_a.at[p], recv_a.at[p], near_edges=p > 0)
        for p in range(parts)
    ]
    latents_of = [
        exchange(latent_out[p], latent_in[p], send_b.at[p], recv_b.at[p])
        for p in range(parts)
    ]
    partials_of = [
        exchange(partial_out.at[s], partial_in.at[s], send_c.at[s], recv_c.at[s], CORES)
        for s in range(slots)
    ]

    for p, (s, first, end) in enumerate(pieces):
        for d in range(n):
            row = (d * slots + s) * heads
            for l in range(lanes):
                absorbed_out[p][d, :, l * LANES : (l + 1) * LANES] = absorbed_rows[
                    l, row + first : row + end, :
                ].astype(jnp.bfloat16)
            if p == 0:
                rotary = [
                    rotary_rows[(d * slots + i) * heads : (d * slots + i + 1) * heads, :]
                    for i in range(slots)
                ]
                absorbed_out[p][d, :, latent:] = jnp.concatenate(rotary, axis=1).astype(jnp.bfloat16)
        if p == 0:
            pl.semaphore_wait(barrier, n - 1)
        queries_of[p][0]()
        absorbed_in[p][me] = absorbed_out[p][me]

    scale = math.log2(math.e) / math.sqrt(width)
    for p, (s, first, end) in enumerate(pieces):
        count = end - first
        rows = n * count
        queries_of[p][1]()
        for i in range(n):
            slot_rows[i * count : (i + 1) * count, :latent] = absorbed_in[p][i, :, :latent].astype(
                jnp.float32
            )
            rotary = absorbed_in[0][i, :, latent:].astype(jnp.float32)
            slot_rows[i * count : (i + 1) * count, latent:] = rotary[
                first:end, s * rope : (s + 1) * rope
            ]
        query = slot_rows[:rows, :].astype(jnp.bfloat16)
        if first == 0:
            load_cache[s].wait()
        length = length_ref[s]
        tops = []
        for t in range(0, context, SCORE_TILE):
            score = jnp.dot(
                query, cache[s, :, t : t + SCORE_TILE], preferred_element_type=jnp.float32
            )
            position = t + lax.broadcasted_iota(jnp.int32, (1, SCORE_TILE), 1)
            score = jnp.where(position < length, score, -jnp.inf)
            scores[:rows, t : t + SCORE_TILE] = score
            tops.append(jnp.max(score, axis=1, keepdims=True))
        highest, total, mixed = None, None, None
        for stage in range(STAGES):
            tiles = range(
                stage * context // STAGES, (stage + 1) * context // STAGES, SCORE_TILE
            )
            top = functools.reduce(jnp.maximum, [tops[t // SCORE_TILE] for t in tiles])
            if highest is not None:
                top = jnp.maximum(highest, top)
                keep = jnp.exp2((highest - top) * scale)
                total, mixed = total * keep, mixed * keep
            highest = top
            for t in tiles:
                prob = jnp.exp2((scores[:rows, t : t + SCORE_TILE] - highest) * scale)
                part = jnp.sum(prob, axis=1, keepdims=True)
                product = lax.dot_general(
                    prob.astype(jnp.bfloat16),
                    cache[s, :latent, t : t + SCORE_TILE],
                    (((1,), (1,)), ((), ())),
                    preferred_element_type=jnp.float32,
                )
                total = part if total is None else total + part
                mixed = product if mixed is None else mixed + product
        mixed = mixed * (1.0 / total)
        for i in range(n):
            latent_out[p][i] = mixed[i * count : (i + 1) * count, :].astype(jnp.bfloat16)
        latents_of[p][0]()
        latent_in[p][me] = latent_out[p][me]

    core, chip = lax.rem(me, CORES), lax.div(me, CORES)
    model = out_ref.shape[1]
    span = model // COLUMNS
    half = span // 2

    def pair(s, k):
        return pltpu.make_async_remote_copy(
            src_ref=partial.at[s, k, CORES - 1 - core],
            dst_ref=partner_rows.at[s, k],
            send_sem=send_p.at[s, k],
            recv_sem=recv_p.at[s, k],
            device_id={"req": me + CORES - 1 - 2 * core},
            device_id_type=MESH,
        )

    waiting = []

    def finish(s, k):
        pair(s, k).wait_recv()
        chip_rows = partial[s, k, core] + partner_rows[s, k]
        for e in range(chips):
            partial_out[s, k, e] = jnp.concatenate(
                [chip_rows[e : e + 1, :half], chip_rows[e : e + 1, half:]], axis=0
            ).astype(jnp.bfloat16)
        partials_of[s][0](k)
        partial_in[s, k, chip] = partial_out[s, k, chip]

    load_value.wait()
    load_weight.wait()
    for p, (s, first, end) in enumerate(pieces):
        count = end - first
        latents_of[p][1]()
        for d in range(n):
            row = ((d % CORES) * chips + d // CORES) * count
            for l in range(lanes):
                returned_rows[l, row : row + count, :] = latent_in[p][
                    d, :, l * LANES : (l + 1) * LANES
                ].astype(jnp.float32)
        values = []
        for h in range(count):
            picked = jnp.concatenate(
                [returned_rows[l, pl.ds(h, n, stride=count), :] for l in range(lanes)], axis=1
            ).astype(jnp.bfloat16)
            values.append(
                jnp.dot(picked, value[first + h], preferred_element_type=jnp.float32).astype(
                    jnp.bfloat16
                )
            )
        values = jnp.concatenate(values, axis=1)
        for k in range(COLUMNS):
            product = jnp.dot(
                values,
                weight[first * vdim : end * vdim, k * span : (k + 1) * span],
                preferred_element_type=jnp.float32,
            )
            if first > 0:
                product = product + carried[:, k * span : (k + 1) * span]
            if end < heads:
                carried[:, k * span : (k + 1) * span] = product
            else:
                for c in range(CORES):
                    partial[s, k, c] = product[c * chips : (c + 1) * chips]
                pair(s, k).start()
                waiting.append((s, k))
            while len(waiting) > 1 or (waiting and end < heads):
                finish(*waiting.pop(0))
    while waiting:
        finish(*waiting.pop(0))

    sums = []
    for s in range(slots):
        partials_of[s][1]()
        for k in range(COLUMNS):
            summed = partial_in[s, k, 0].astype(jnp.float32)
            for e in range(1, chips):
                summed = summed + partial_in[s, k, e].astype(jnp.float32)
            sums.append(summed)
    for k in range(COLUMNS):
        for c in range(2):
            at = k * span + c * half
            out_ref[:, at : at + half] = jnp.concatenate(
                [summed[c : c + 1] for summed in sums[k::COLUMNS]], axis=0
            ).astype(jnp.bfloat16)
    for s in range(slots):
        for k in range(COLUMNS):
            pair(s, k).wait_send()
    for pending in queries_of + latents_of + partials_of:
        pending[2]()


def on_device(n, queries, absorb_key, absorb_value, out_weight, latent_cache, lengths, slot_request):
    cache = jnp.swapaxes(latent_cache, 1, 2)
    requests, heads, width = queries.shape
    slots, key_width, context = cache.shape
    nope, latent = absorb_key.shape[1:]
    model = out_weight.shape[1]
    rows = requests * heads
    chips = n // CORES
    pieces = pieces_of(slots, heads)
    span = model // COLUMNS
    vmem, anywhere = (pl.BlockSpec(memory_space=space) for space in (pltpu.VMEM, pltpu.HBM))
    low, wide = jnp.bfloat16, jnp.float32
    absorbed = [
        pltpu.VMEM((n, end - first, latent + (slots * (width - nope) if p == 0 else 0)), low)
        for p, (_, first, end) in enumerate(pieces)
    ]
    mixed = [pltpu.VMEM((n, end - first, latent), low) for _, first, end in pieces]
    per_piece = pltpu.SemaphoreType.DMA((len(pieces),))
    return pl.pallas_call(
        functools.partial(kernel, n, pieces),
        out_shape=jax.ShapeDtypeStruct((slots, model), low),
        in_specs=[anywhere] * 7,
        out_specs=vmem,
        scratch_shapes=[
            pltpu.SMEM(slot_request.shape, jnp.int32),
            pltpu.SMEM(lengths.shape, jnp.int32),
            pltpu.VMEM(queries.shape, low),
            pltpu.VMEM(absorb_key.shape, low),
            pltpu.VMEM(absorb_value.shape, low),
            pltpu.VMEM(out_weight.shape, low),
            pltpu.VMEM(cache.shape, low),
            pltpu.VMEM((rows, nope), wide),
            pltpu.VMEM((rows, width - nope), wide),
            pltpu.VMEM((latent // LANES, rows, LANES), wide),
            pltpu.VMEM((n * heads, key_width), wide),
            pltpu.VMEM((n * heads, context), wide),
            pltpu.VMEM((n * heads, latent), wide),
            pltpu.VMEM((latent // LANES, n * heads, LANES), wide),
            *absorbed,
            *absorbed,
            *mixed,
            *mixed,
            pltpu.VMEM((n, model), wide),
            pltpu.VMEM((slots, COLUMNS, CORES, chips, span), wide),
            pltpu.VMEM((slots, COLUMNS, chips, span), wide),
            pltpu.VMEM((slots, COLUMNS, chips, 2, span // 2), low),
            pltpu.VMEM((slots, COLUMNS, chips, 2, span // 2), low),
            pltpu.SemaphoreType.DMA((3,)),
            pltpu.SemaphoreType.DMA((3 + slots,)),
            per_piece,
            per_piece,
            per_piece,
            per_piece,
            pltpu.SemaphoreType.DMA((slots, COLUMNS)),
            pltpu.SemaphoreType.DMA((slots, COLUMNS)),
            pltpu.SemaphoreType.DMA((slots,)),
            pltpu.SemaphoreType.DMA((slots,)),
        ],
        compiler_params=pltpu.CompilerParams(
            collective_id=0, has_side_effects=True, vmem_limit_bytes=56000 * 1000
        ),
        name="decode",
    )(
        *(
            pltpu.with_memory_space_constraint(operand, pltpu.HBM)
            for operand in (slot_request, lengths, queries, absorb_key, absorb_value, out_weight, cache)
        )
    )


def solution(mesh):
    return jax.shard_map(
        functools.partial(on_device, mesh.shape["req"]),
        mesh=mesh,
        in_specs=(
            P("groups", "req", None),
            P("req", None, None),
            P("req", None, None),
            P("req", None),
            P(("groups", "req"), None, None),
            P(("groups", "req")),
            P("groups"),
        ),
        out_specs=P(("groups", "req"), None),
        check_vma=False,
    )
```
